32 devices in a mesh: req: 4 (over z), exp: 8 (over y, x, core).
Axes of the slice: x: 2, y: 2, z: 4, core: 2. Of those that a mesh axis runs over, the one named last changes fastest.
Arguments:
- queries: bfloat16 [64, 32, 2304], P(('req', 'exp')), may hold values from -8 to 8
- draft_keys: bfloat16 [64, 32, 2304], P(('req', 'exp')), may hold values from -9 to 9
- draft_values: bfloat16 [64, 32, 2304], P(('req', 'exp')), may hold values from -6 to 6
- tree_parents: int32 [64, 32], P(('req', 'exp')), may hold values from -1 to 30, as said below
- cache_keys: bfloat16 [64, 768, 2304], P(('req', 'exp')), may hold values from -9 to 9
- cache_values: bfloat16 [64, 768, 2304], P(('req', 'exp')), may hold values from -6 to 6
- cache_lengths: int32 [64], P(('req', 'exp')), may hold values from 1 to 768, as said below
- prompt_keys: bfloat16 [8, 512, 2304], P('req', 'exp'), may hold values from -9 to 9
- prompt_values: bfloat16 [8, 512, 2304], P('req', 'exp'), may hold values from -6 to 6
- group_ids: int32 [64], P(('req', 'exp')), may hold values from 0 to 1
- residual: bfloat16 [64, 32, 2304], P(('req', 'exp')), may hold values from -6 to 6
- norm_gain: float32 [2304], replicated, may hold values from 0.5 to 1.5
- router: bfloat16 [2304, 8], replicated, may hold values from -0.125 to 0.125
- w_gate: bfloat16 [8, 2304, 5760], P('exp', None, 'req'), may hold values from -0.125 to 0.125
- w_up: bfloat16 [8, 2304, 5760], P('exp', None, 'req'), may hold values from -0.125 to 0.125
- w_down: bfloat16 [8, 5760, 2304], P('exp', 'req'), may hold values from -0.078125 to 0.078125
- expert_ids: int32 [64, 32, 2], P(('req', 'exp')), may hold values from 0 to 7, all different within a row; in each aligned block of 64 rows (0 to 63, 64 to 127, ..., all dimensions but the last counted through in order) at most 18 rows name the same one
- accepted_rows: int32 [64, 8], P(('req', 'exp')), may hold values from 0 to 31
Outputs:
- attended: bfloat16 [64, 32, 2304], P(('req', 'exp'))
- layer_out: bfloat16 [64, 32, 2304], P(('req', 'exp'))
- accepted_cache: bfloat16 [64, 2, 8, 2304], P(('req', 'exp'))
The draws below stay inside these ranges and needn't reach their ends.
Inputs may be any that keep to these rules, and one draw needn't show every extreme that they name: `tree_parents`: position 0 of every tree holds -1; every other position holds an earlier position of the same tree. `cache_lengths`: some request has all 768 slots used. `expert_ids`: the two experts of a position differ; among the rows of one device no expert is named more than 18 times, a bound that some block reaches.
All inputs are finite; a program needn't handle non-finite values.
Results may differ from the reference program's by a relative error of at most 0.013.
Values may be sent and summed in bfloat16 or wider, within the bound.
A program may use at most 192 MiB of HBM per device.

```python
import math
import jax
import jax.numpy as jnp
import numpy as np
from jax import lax

D = 2304
HEADS = 36
HDIM = 64
EXPERTS = 8
FF = 5760
TOPK = 2
TREE = 32
CACHE = 768
GRP = 2
PATH = 8
ROWS = 64
CAP = 18
ROW_REQS = 16
REQS = 64
PROMPT = 512
GROUPS = 8
HOLD = 1
FFH = 5760
FFD = 1440
N_REQ = 4
N_EXP = 8


def draw_queries(key, part):
    extent = (REQS, TREE, D)
    values = jnp.clip(1.5 * jax.random.normal(jax.random.fold_in(key, 1), extent, jnp.float32), -8.0, 8.0)
    return values.astype(jnp.bfloat16)


def draw_prompt_keys(key, part):
    extent = (GROUPS, PROMPT, D)
    values = jnp.clip(1.5 * jax.random.normal(jax.random.fold_in(key, 2), extent, jnp.float32), -9.0, 9.0)
    return values.astype(jnp.bfloat16)


def draw_cache_lengths(key, part):
    lengths = jax.random.randint(jax.random.fold_in(key, 3), (REQS,), 1, CACHE + 1)
    filled = jax.random.randint(jax.random.fold_in(key, 4), (), 0, REQS)
    return lengths.at[filled].set(CACHE).astype(jnp.int32)


def draw_tree_parents(key, part):
    position = jnp.arange(TREE, dtype=jnp.int32)[None, :]
    offset = jax.random.randint(jax.random.fold_in(key, 5), (REQS, TREE), 1, 5)
    parents = jnp.maximum(position - offset, 0)
    return jnp.where(position == 0, -1, parents).astype(jnp.int32)


def place_ends(values, stream_key, least, high):
    longest = values.shape.index(max(values.shape))
    spots = []
    for shift in (0, 1):
        where = [jax.random.randint(jax.random.fold_in(stream_key, axis), (), 0, length) for axis, length in enumerate(values.shape)]
        where[longest] = (where[longest] + shift) % values.shape[longest]
        spots.append(tuple(where))
    return values.at[spots[0]].set(least).at[spots[1]].set(high)


def steps_of(key, dims, shards, smallest, top_value):
    factor_of, own = 1.0, jax.random.fold_in(key, 6)
    for axis_at, blocks in shards:
        steps = jnp.exp(jax.random.uniform(jax.random.fold_in(own, axis_at), (blocks,), jnp.float32, smallest / len(shards), top_value / len(shards)))
        factor_of = factor_of * jnp.repeat(steps, dims[axis_at] // blocks).reshape([-1 if axis == axis_at else 1 for axis in range(len(dims))])
    return factor_of


def deal_out(key, own, number, rows, count, top, most, slope):
    sequence = jax.random.permutation(key, count)
    heavy_load, ordinary = shares(count, rows * top, most, slope, True), shares(count, rows * top, most, slope, False)
    places = jnp.arange(count)

    def named(tallies, offset_by):
        used = int((tallies > 0).sum())
        fixed = max(1, used // 4)
        shifted = fixed + (places - fixed + offset_by * (used - fixed)) % max(1, count - fixed)
        return jnp.zeros((count,), jnp.int32).at[sequence[jnp.where(places < fixed, places, shifted)]].set(jnp.asarray(tallies, jnp.int32))

    tallies = jnp.where(number % 4 == 0, named(heavy_load, number // 4), named(ordinary, number - number // 4 - 1))
    mixed = jax.random.permutation(jax.random.fold_in(own, 3), count)
    source_of, taker = mixed[0:count // 2 * 2:2], mixed[1:count // 2 * 2:2]
    room = jnp.minimum(tallies[source_of] - 1, most - tallies[taker]) // 2
    room = jnp.where((source_of == sequence[0]) | (taker == sequence[0]) | (tallies[taker] == 0), 0, jnp.maximum(room, 0))
    shifted = jax.random.randint(jax.random.fold_in(own, 4), (count // 2,), 0, 1 << 20) % (room + 1)
    tallies = tallies.at[source_of].add(-shifted).at[taker].add(shifted)
    labels = jnp.searchsorted(jnp.cumsum(tallies), jnp.arange(rows * top), side="right").astype(jnp.int32)
    listing = labels.reshape(top, rows).T
    listing = listing[jax.random.permutation(jax.random.fold_in(own, 1), rows)]
    offset_by = jax.random.randint(jax.random.fold_in(own, 2), (rows, 1), 0, top)
    return jnp.take_along_axis(listing, (jnp.arange(top)[None, :] + offset_by) % top, axis=1)


def shares(number_of, total, most, skew, full):
    loads = [(1 << 20) // math.isqrt(standing ** skew) + 1 for standing in range(1, number_of + 1)]
    largest = most if full else min(most, max(-(-total // number_of), total * loads[0] // sum(loads)))
    least = 1 if total - largest >= number_of - 1 else 0
    holding, spare = [largest] + [least] * (number_of - 1), total - largest - least * (number_of - 1)
    while spare > 0:
        movable = [i for i in range(1, number_of) if holding[i] < largest] or [i for i in range(1, number_of) if holding[i] < most]
        mass, budget = sum([loads[i] for i in movable]), spare
        for i in movable:
            more = min(most - holding[i], max(1, budget * loads[i] // mass), spare)
            holding[i] = holding[i] + more
            spare = spare - more
    return np.array(holding)


def centred(stream_key, shape, width, most, cuts=(), kind=jnp.bfloat16):
    factor_of = steps_of(stream_key, shape, cuts, -0.22, 0.18) if cuts else 1.0
    result = jax.random.normal(stream_key, shape, jnp.float32) * width * factor_of
    return jnp.minimum(jnp.maximum(result, -most), most).astype(kind)


def setup_inputs(seed: int = 0) -> dict:
    key_of = jax.random.split(jax.random.key(seed), 19)
    queries = draw_queries(jax.random.fold_in(key_of[18], 71), 0)
    draft_keys = centred(key_of[1], (REQS, TREE, D), 1.5, 9.0, ((0, 32),))
    draft_values = centred(key_of[2], (REQS, TREE, D), 1.0, 6.0, ((0, 32),))
    tree_parents = draw_tree_parents(jax.random.fold_in(key_of[18], 71), 0)
    cache_keys = centred(key_of[4], (REQS, CACHE, D), 1.5, 9.0, ((0, 32),))
    cache_values = centred(key_of[5], (REQS, CACHE, D), 1.0, 6.0, ((0, 32),))
    cache_lengths = draw_cache_lengths(jax.random.fold_in(key_of[18], 71), 0)
    prompt_keys = draw_prompt_keys(jax.random.fold_in(key_of[18], 71), 0)
    prompt_values = centred(key_of[8], (GROUPS, PROMPT, D), 1.0, 6.0, ((0, 4), (1, 8)))
    group_ids = place_ends(jax.random.randint(key_of[9], (REQS,), 0, GRP), jax.random.fold_in(key_of[9], 1), 0, GRP - 1).astype(jnp.int32)
    residual = centred(key_of[10], (REQS, TREE, D), 1.0, 6.0, ((0, 32),))
    norm_gain = jnp.clip(1.0 + 0.1 * jax.random.normal(key_of[11], (D,), jnp.float32), 0.5, 1.5)
    router = centred(key_of[12], (D, EXPERTS), D ** -0.5, 0.125)
    w_gate = centred(key_of[13], (N_EXP, D, FFH), D ** -0.5, 0.125, ((0, 8), (2, 4)))
    w_up = centred(key_of[14], (N_EXP, D, FFH), D ** -0.5, 0.125, ((0, 8), (2, 4)))
    w_down = centred(key_of[15], (N_EXP, FFH, D), FF ** -0.5, 0.078125, ((0, 8), (1, 4)))
    expert_ids_keys = jax.random.split(jax.random.fold_in(key_of[16], 1), REQS * TREE // ROWS)
    expert_ids_turns = jax.random.permutation(jax.random.fold_in(key_of[16], 3), REQS * TREE // ROWS)
    expert_ids = jax.vmap(lambda own, number: deal_out(jax.random.fold_in(key_of[16], 2), own, number, ROWS, EXPERTS, TOPK, CAP, 1))(expert_ids_keys, expert_ids_turns).reshape((REQS, TREE, TOPK))
    accepted_rows = place_ends(jax.random.randint(key_of[17], (REQS, PATH), 0, TREE), jax.random.fold_in(key_of[17], 1), 0, TREE - 1).astype(jnp.int32)
    return {"queries": queries, "draft_keys": draft_keys, "draft_values": draft_values, "tree_parents": tree_parents, "cache_keys": cache_keys, "cache_values": cache_values, "cache_lengths": cache_lengths, "prompt_keys": prompt_keys, "prompt_values": prompt_values, "group_ids": group_ids, "residual": residual, "norm_gain": norm_gain, "router": router, "w_gate": w_gate, "w_up": w_up, "w_down": w_down, "expert_ids": expert_ids, "accepted_rows": accepted_rows}


HIGH = lax.Precision.HIGHEST
EPSILON = 1e-05

def ancestry(parents):
    length = parents.shape[-1]
    column = jnp.arange(length, dtype=jnp.int32)
    reached = (parents[..., :, None] == column).astype(jnp.float32) + jnp.eye(length, dtype=jnp.float32)
    for repeat in range(max(1, (length - 1).bit_length())):
        reached = (jnp.einsum('...ij,...jk->...ik', reached, reached, precision=HIGH) > 0.5).astype(jnp.float32)
    return reached > 0.5

def slot_numbers(picked_ids):
    flattened = picked_ids.reshape(-1)
    onehot = (flattened[:, None] == jnp.arange(EXPERTS, dtype=jnp.int32)[None, :]).astype(jnp.int32)
    before = jnp.cumsum(onehot, axis=0) - onehot
    return lax.optimization_barrier(jnp.sum(before * onehot, axis=1)).reshape(picked_ids.shape)

def reference(queries, draft_keys, draft_values, tree_parents, cache_keys, cache_values, cache_lengths, prompt_keys, prompt_values, group_ids, residual, norm_gain, router, w_gate, w_up, w_down, expert_ids, accepted_rows):
    home = jnp.arange(REQS, dtype=jnp.int32) // ROW_REQS * GRP + group_ids
    score_scale = HDIM ** (-0.5)

    def attend_request(inputs):
        query, group, length, cache_k, cache_v, draft_k, draft_v, parents = inputs
        heads_q = query.astype(jnp.float32).reshape(TREE, HEADS, HDIM)
        keys_all = jnp.concatenate([prompt_keys[group], cache_k, draft_k], 0).astype(jnp.float32).reshape(-1, HEADS, HDIM)
        values_all = jnp.concatenate([prompt_values[group], cache_v, draft_v], 0).astype(jnp.float32).reshape(-1, HEADS, HDIM)
        scores = jnp.einsum('thd,khd->thk', heads_q, keys_all) * score_scale
        live_cache = jnp.arange(CACHE, dtype=jnp.int32) < length
        visible = jnp.concatenate([jnp.ones((TREE, PROMPT), jnp.bool_), jnp.broadcast_to(live_cache[None, :], (TREE, CACHE)), ancestry(parents)], 1)
        scores = jnp.where(visible[:, None, :], scores, -jnp.inf)
        highest = lax.optimization_barrier(jnp.max(scores, axis=-1, keepdims=True))
        weights = jnp.exp(scores - highest)
        total = lax.optimization_barrier(jnp.sum(weights, axis=-1))
        rounded = lax.optimization_barrier(weights.astype(jnp.bfloat16)).astype(jnp.float32)
        mixed = jnp.einsum('thk,khd->thd', rounded, values_all) / total[..., None]
        return mixed.reshape(TREE, D).astype(jnp.bfloat16)
    attended = lax.map(attend_request, (queries, home, cache_lengths, cache_keys, cache_values, draft_keys, draft_values, tree_parents))
    stream = (residual.astype(jnp.float32) + attended.astype(jnp.float32)).astype(jnp.bfloat16)
    rows_in = stream.reshape(-1, D).astype(jnp.float32)
    normed = (rows_in * lax.rsqrt(lax.optimization_barrier(jnp.mean(rows_in * rows_in, axis=-1, keepdims=True)) + EPSILON) * norm_gain).astype(jnp.bfloat16)
    logits = jnp.dot(normed, router, preferred_element_type=jnp.float32)
    chosen = jnp.take_along_axis(logits, expert_ids.reshape(-1, TOPK), axis=1)
    gate_first = 1.0 / (1.0 + jnp.exp(chosen[:, 1] - chosen[:, 0]))
    gates = jnp.stack([gate_first, 1.0 - gate_first], axis=1)
    blocks = N_REQ * N_EXP
    picked_ids = expert_ids.reshape(blocks, ROWS, TOPK)
    slots = jax.vmap(slot_numbers)(picked_ids)
    block_rows = normed.reshape(blocks, ROWS, D)

    def fill_block(rows_here, ids_here, slots_here):
        target = (ids_here * CAP + slots_here).reshape(-1)
        return jnp.zeros((EXPERTS * CAP, D), jnp.bfloat16).at[target].set(jnp.repeat(rows_here, TOPK, axis=0))
    buffers = jax.vmap(fill_block)(block_rows, picked_ids, slots)
    buffers = buffers.reshape(blocks, EXPERTS, CAP, D).transpose(1, 0, 2, 3).reshape(EXPERTS, blocks * CAP, D)
    gate_full = w_gate.reshape(EXPERTS, HOLD, D, FFH).transpose(0, 2, 1, 3).reshape(EXPERTS, D, FF)
    up_full = w_up.reshape(EXPERTS, HOLD, D, FFH).transpose(0, 2, 1, 3).reshape(EXPERTS, D, FF)
    down_full = w_down.reshape(EXPERTS, HOLD, FFH // FFD, FFD, D)

    def expert_out(inputs):
        rows_here, gate_w, up_w, down_w = inputs
        gate_proj = jnp.dot(rows_here, gate_w, preferred_element_type=jnp.float32)
        up_proj = jnp.dot(rows_here, up_w, preferred_element_type=jnp.float32)
        act = (jax.nn.silu(gate_proj) * up_proj).astype(jnp.bfloat16)
        act = act.reshape(rows_here.shape[0], HOLD, FFH // FFD, FFD).astype(jnp.float32)
        parts = jnp.einsum('nhrf,hrfd->hrnd', act, down_w.astype(jnp.float32))
        parts = lax.optimization_barrier(parts.astype(jnp.bfloat16)).astype(jnp.float32)
        holder = lax.optimization_barrier(lax.optimization_barrier(jnp.sum(parts, axis=1)).astype(jnp.bfloat16)).astype(jnp.float32)
        return lax.optimization_barrier(jnp.sum(holder, axis=0))
    outputs = lax.map(expert_out, (buffers, gate_full, up_full, down_full))
    block_index = jnp.arange(blocks, dtype=jnp.int32)[:, None, None]
    index = ((picked_ids * blocks + block_index) * CAP + slots).reshape(-1, TOPK).astype(jnp.int32)
    picked = outputs.reshape(-1, D)[index]
    layer_out = (rows_in + lax.optimization_barrier(jnp.sum(gates[:, :, None] * picked, axis=1))).astype(jnp.bfloat16).reshape(REQS, TREE, D)
    kept_keys = jnp.take_along_axis(draft_keys, accepted_rows[:, :, None], axis=1)
    kept_values = jnp.take_along_axis(draft_values, accepted_rows[:, :, None], axis=1)
    accepted_cache = jnp.stack([kept_keys, kept_values], axis=1)
    return (attended, layer_out, accepted_cache)
```

```python
import jax
import jax.numpy as jnp
from jax import lax
from jax.experimental import pallas as pl
from jax.experimental.pallas import tpu as pltpu
from jax.sharding import PartitionSpec as P

HEADS = 36
HDIM = 64
EXPERTS = 8
TOPK = 2
GRP = 2
CAP = 18
LANES = 256
PACK = LANES // HDIM
STAT = 128


HIGH = lax.Precision.HIGHEST
EPSILON = 1e-05


def ancestry(parents):
    length = parents.shape[-1]
    column = jnp.arange(length, dtype=jnp.int32)
    reached = (parents[..., :, None] == column).astype(jnp.float32) + jnp.eye(
        length, dtype=jnp.float32
    )
    for repeat in range(max(1, (length - 1).bit_length())):
        reached = (jnp.einsum("...ij,...jk->...ik", reached, reached, precision=HIGH) > 0.5).astype(
            jnp.float32
        )
    return reached > 0.5


def slot_numbers(picked_ids):
    flattened = picked_ids.reshape(-1)
    onehot = (flattened[:, None] == jnp.arange(EXPERTS, dtype=jnp.int32)[None, :]).astype(jnp.int32)
    before = jnp.cumsum(onehot, axis=0) - onehot
    return jnp.sum(before * onehot, axis=1).reshape(picked_ids.shape)


SCALE = HDIM ** (-0.5)
NT = (((1,), (1,)), ((), ()))


def head_masks(rows):
    head = lax.broadcasted_iota(jnp.int32, (rows, LANES), 1) // HDIM
    return [(head == h).astype(jnp.float32).astype(jnp.bfloat16) for h in range(PACK)]


def local_kernel(len_ref, q_ref, kc_ref, vc_ref, kd_ref, vd_ref, anc_ref, acc_ref, stat_ref):
    b, g = pl.program_id(0), pl.program_id(1)
    tree = q_ref.shape[1]
    q = q_ref[0]
    masks = head_masks(tree)
    stacked = jnp.concatenate([q * mask for mask in masks], axis=0)
    s_cache = lax.dot_general(stacked, kc_ref[0], NT, preferred_element_type=jnp.float32) * SCALE
    slot = lax.broadcasted_iota(jnp.int32, s_cache.shape, 1)
    s_cache = jnp.where(slot < len_ref[b], s_cache, -jnp.inf)
    s_tree = lax.dot_general(stacked, kd_ref[0], NT, preferred_element_type=jnp.float32) * SCALE
    anc = jnp.concatenate([anc_ref[0]] * PACK, axis=0)
    s_tree = jnp.where(anc > 0.5, s_tree, -jnp.inf)
    top = jnp.maximum(
        jnp.max(s_cache, axis=1, keepdims=True), jnp.max(s_tree, axis=1, keepdims=True)
    )
    w_cache = jnp.exp(s_cache - top)
    w_tree = jnp.exp(s_tree - top)
    total = jnp.sum(w_cache, axis=1, keepdims=True) + jnp.sum(w_tree, axis=1, keepdims=True)
    mixed = jnp.dot(w_cache.astype(jnp.bfloat16), vc_ref[0], preferred_element_type=jnp.float32)
    mixed += jnp.dot(w_tree.astype(jnp.bfloat16), vd_ref[0], preferred_element_type=jnp.float32)
    head = lax.broadcasted_iota(jnp.int32, (tree, LANES), 1) // HDIM
    lane = lax.broadcasted_iota(jnp.int32, (tree, STAT), 1)

    @pl.when(g == 0)
    def _():
        stat_ref[...] = jnp.zeros_like(stat_ref)

    out = jnp.zeros((tree, LANES), jnp.float32)
    stat = stat_ref[0]
    for h in range(PACK):
        rows = slice(h * tree, (h + 1) * tree)
        out = jnp.where(head == h, mixed[rows], out)
        stat = jnp.where(lane == g * PACK + h, top[rows], stat)
        stat = jnp.where(lane == STAT // 2 + g * PACK + h, total[rows], stat)
    acc_ref[0] = out
    stat_ref[0] = stat


def prompt_kernel(q_ref, group_ref, k_ref, v_ref, acc_ref, stat_ref):
    g = pl.program_id(0)
    sources, rows = q_ref.shape[0], q_ref.shape[1]
    groups, positions = k_ref.shape[0], k_ref.shape[1]
    keys = groups * positions
    k = k_ref[...].reshape(keys, LANES)
    v = v_ref[...].reshape(keys, LANES)
    masks = head_masks(keys)
    k_wide = jnp.concatenate([k * mask for mask in masks], axis=0)
    v_wide = jnp.concatenate([v * mask for mask in masks], axis=0)
    key_group = (lax.broadcasted_iota(jnp.int32, (rows, keys), 1) // positions).astype(jnp.float32)
    lane = lax.broadcasted_iota(jnp.int32, (rows, STAT), 1)

    @pl.when(g == 0)
    def _():
        stat_ref[...] = jnp.zeros_like(stat_ref)

    for s in range(sources):
        scores = lax.dot_general(q_ref[s], k_wide, NT, preferred_element_type=jnp.float32) * SCALE
        live = key_group == group_ref[s].astype(jnp.float32)[:, :1]
        stat = stat_ref[s]
        weights = []
        for h in range(PACK):
            part = jnp.where(live, scores[:, h * keys : (h + 1) * keys], -jnp.inf)
            top = jnp.max(part, axis=1, keepdims=True)
            weight = jnp.exp(part - top)
            stat = jnp.where(lane == g * PACK + h, top, stat)
            stat = jnp.where(
                lane == STAT // 2 + g * PACK + h, jnp.sum(weight, axis=1, keepdims=True), stat
            )
            weights.append(weight.astype(jnp.bfloat16))
        stat_ref[s] = stat
        acc_ref[s] = jnp.dot(
            jnp.concatenate(weights, axis=1), v_wide, preferred_element_type=jnp.float32
        ).astype(jnp.bfloat16)


def merge_kernel(
    part_ref, pstat_ref, acc_ref, stat_ref, residual_ref, gain_ref, att_ref, stream_ref, normed_ref
):
    sources, rows, width = part_ref.shape
    stats = [stat_ref[...]] + [pstat_ref[s] for s in range(sources)]
    top = stats[0]
    for stat in stats[1:]:
        top = jnp.maximum(top, stat)
    scales = [jnp.exp(stat - top) for stat in stats]
    total = sum(scale * pltpu.roll(stat, STAT // 2, 1) for scale, stat in zip(scales, stats))
    scales = [scale / total for scale in scales]
    squares = jnp.zeros((rows, 1), jnp.float32)
    left = lax.broadcasted_iota(jnp.int32, (rows, STAT), 1) < HDIM
    for pair in range(width // STAT):
        cols = slice(pair * STAT, (pair + 1) * STAT)
        a = 2 * pair
        out = jnp.zeros((rows, STAT), jnp.float32)
        for i in range(sources + 1):
            values = acc_ref[:, cols] if i == 0 else part_ref[i - 1, :, cols].astype(jnp.float32)
            out += values * jnp.where(left, scales[i][:, a : a + 1], scales[i][:, a + 1 : a + 2])
        attended = out.astype(jnp.bfloat16)
        att_ref[:, cols] = attended
        stream = (
            residual_ref[:, cols].astype(jnp.float32) + attended.astype(jnp.float32)
        ).astype(jnp.bfloat16)
        stream_ref[:, cols] = stream
        stream = stream.astype(jnp.float32)
        squares += jnp.sum(stream * stream, axis=1, keepdims=True)
    factor = lax.rsqrt(squares / width + EPSILON)
    normed_ref[...] = (
        stream_ref[...].astype(jnp.float32) * factor * gain_ref[...]
    ).astype(jnp.bfloat16)


def attention(
    queries, draft_keys, draft_values, tree_parents, cache_keys, cache_values, cache_lengths,
    prompt_keys, prompt_values, group_ids, residual, norm_gain,
):
    requests, tree, width = queries.shape
    rows, packs, cache = requests * tree, width // LANES, cache_keys.shape[1]
    groups, positions = prompt_keys.shape[:2]
    row_group = jnp.broadcast_to(
        jnp.repeat(group_ids, tree)[:, None].astype(jnp.bfloat16), (rows, STAT)
    )
    sent = jnp.concatenate([queries.reshape(rows, width), row_group], axis=1)
    plane = lax.all_gather(sent, "exp", axis=0, tiled=False)
    sources = plane.shape[0]
    anc = ancestry(tree_parents).astype(jnp.float32)
    block = lambda n: pl.BlockSpec((1, n, LANES), lambda b, g, _: (b, 0, g))
    flops = 4 * rows * PACK * width * (cache + tree)
    acc, stat = pl.pallas_call(
        local_kernel,
        grid_spec=pltpu.PrefetchScalarGridSpec(
            num_scalar_prefetch=1,
            grid=(requests, packs),
            in_specs=[
                block(tree), block(cache), block(cache), block(tree), block(tree),
                pl.BlockSpec((1, tree, tree), lambda b, g, _: (b, 0, 0)),
            ],
            out_specs=[block(tree), pl.BlockSpec((1, tree, STAT), lambda b, g, _: (b, 0, 0))],
        ),
        out_shape=[
            jax.ShapeDtypeStruct((requests, tree, width), jnp.float32),
            jax.ShapeDtypeStruct((requests, tree, STAT), jnp.float32),
        ],
        cost_estimate=pl.CostEstimate(
            flops=flops, bytes_accessed=4 * requests * cache * width,
            transcendentals=rows * HEADS * cache,
        ),
        name="local_attention",
    )(cache_lengths, queries, cache_keys, cache_values, draft_keys, draft_values, anc)
    pblock = pl.BlockSpec((groups, positions, LANES), lambda g: (0, 0, g))
    part, pstat = pl.pallas_call(
        prompt_kernel,
        grid=(packs,),
        in_specs=[
            pl.BlockSpec((sources, rows, LANES), lambda g: (0, 0, g)),
            pl.BlockSpec((sources, rows, STAT), lambda g: (0, 0, width // STAT)),
            pblock,
            pblock,
        ],
        out_specs=[
            pl.BlockSpec((sources, rows, LANES), lambda g: (0, 0, g)),
            pl.BlockSpec((sources, rows, STAT), lambda g: (0, 0, 0)),
        ],
        out_shape=[
            jax.ShapeDtypeStruct((sources, rows, width), jnp.bfloat16),
            jax.ShapeDtypeStruct((sources, rows, STAT), jnp.float32),
        ],
        name="prompt_attention",
    )(plane, plane, prompt_keys, prompt_values)
    part = lax.all_to_all(part, "exp", split_axis=0, concat_axis=0, tiled=True)
    pstat = lax.all_to_all(pstat, "exp", split_axis=0, concat_axis=0, tiled=True)
    return pl.pallas_call(
        merge_kernel,
        out_shape=[jax.ShapeDtypeStruct((rows, width), jnp.bfloat16)] * 3,
        compiler_params=pltpu.CompilerParams(vmem_limit_bytes=32 * 1024 * 1024),
        name="merge",
    )(
        part, pstat, acc.reshape(rows, width), stat.reshape(rows, STAT),
        residual.reshape(rows, width), norm_gain.reshape(1, width),
    )


def on_device(
    queries,
    draft_keys,
    draft_values,
    tree_parents,
    cache_keys,
    cache_values,
    cache_lengths,
    prompt_keys,
    prompt_values,
    group_ids,
    residual,
    norm_gain,
    router,
    w_gate,
    w_up,
    w_down,
    expert_ids,
    accepted_rows,
):
    requests, tree_len, width = queries.shape
    row_count = requests * tree_len
    attended, stream, normed = attention(
        queries, draft_keys, draft_values, tree_parents, cache_keys, cache_values, cache_lengths,
        prompt_keys, prompt_values, group_ids, residual, norm_gain,
    )
    attended = attended.reshape(requests, tree_len, width)
    stream_rows = stream.astype(jnp.float32)
    logits = jnp.dot(normed, router, preferred_element_type=jnp.float32)
    routed = expert_ids.reshape(row_count, TOPK)
    chosen = jnp.take_along_axis(logits, routed, axis=1)
    gate_first = 1.0 / (1.0 + jnp.exp(chosen[:, 1] - chosen[:, 0]))
    gates = jnp.stack([gate_first, 1.0 - gate_first], axis=1)
    target = routed * CAP + slot_numbers(routed)
    buffer = (
        jnp.zeros((EXPERTS * CAP, width), jnp.bfloat16)
        .at[target.reshape(-1)]
        .set(jnp.repeat(normed, TOPK, axis=0))
    )
    holder_count = lax.axis_size("exp")
    holders = holder_count // EXPERTS
    outgoing = jnp.broadcast_to(
        buffer.reshape(EXPERTS, 1, CAP, width), (EXPERTS, holders, CAP, width)
    ).reshape(holder_count, CAP, width)
    gate_local = w_gate[0]
    up_local = w_up[0]
    down_local = w_down[0]
    arrived = lax.all_to_all(outgoing, "exp", split_axis=0, concat_axis=0, tiled=True)
    row_piece = lax.all_gather(arrived.reshape(-1, width), "req", axis=0, tiled=True)
    gate_proj = jnp.dot(row_piece, gate_local, preferred_element_type=jnp.float32)
    up_proj = jnp.dot(row_piece, up_local, preferred_element_type=jnp.float32)
    hidden = (jax.nn.silu(gate_proj) * up_proj).astype(jnp.bfloat16)
    summed_rows = lax.psum_scatter(
        jnp.dot(hidden, down_local, preferred_element_type=jnp.float32).astype(jnp.bfloat16),
        "req",
        scatter_dimension=0,
        tiled=True,
    )
    returned = lax.all_to_all(
        summed_rows.reshape(holder_count, CAP, width),
        "exp",
        split_axis=0,
        concat_axis=0,
        tiled=True,
    )
    expert_result = (
        returned.astype(jnp.float32)
        .reshape(EXPERTS, holders, CAP, width)
        .sum(axis=1)
        .reshape(EXPERTS * CAP, width)
    )
    picked = expert_result[target]
    layer_out = (
        (stream_rows + jnp.sum(gates[:, :, None] * picked, axis=1))
        .astype(jnp.bfloat16)
        .reshape(requests, tree_len, width)
    )
    kept_keys = jnp.take_along_axis(draft_keys, accepted_rows[:, :, None], axis=1)
    kept_values = jnp.take_along_axis(draft_values, accepted_rows[:, :, None], axis=1)
    accepted_cache = jnp.stack([kept_keys, kept_values], axis=1)
    return (attended, layer_out, accepted_cache)


def solution(mesh):
    return jax.shard_map(
        on_device,
        mesh=mesh,
        in_specs=(
            P(("req", "exp"), None, None),
            P(("req", "exp"), None, None),
            P(("req", "exp"), None, None),
            P(("req", "exp"), None),
            P(("req", "exp"), None, None),
            P(("req", "exp"), None, None),
            P(("req", "exp")),
            P("req", "exp", None),
            P("req", "exp", None),
            P(("req", "exp")),
            P(("req", "exp"), None, None),
            P(),
            P(),
            P("exp", None, "req"),
            P("exp", None, "req"),
            P("exp", "req", None),
            P(("req", "exp"), None, None),
            P(("req", "exp"), None),
        ),
        out_specs=(
            P(("req", "exp"), None, None),
            P(("req", "exp"), None, None),
            P(("req", "exp"), None, None, None),
        ),
        check_vma=False,
    )
```

```python
import functools

import jax
import jax.numpy as jnp
from jax import lax
from jax.experimental import pallas as pl
from jax.experimental.pallas import tpu as pltpu
from jax.sharding import PartitionSpec as P

HEADS = 36
HDIM = 64
EXPERTS = 8
TOPK = 2
GRP = 2
CAP = 18
LANES = 256
PACK = LANES // HDIM
STAT = 128


HIGH = lax.Precision.HIGHEST
EPSILON = 1e-05


def ancestry(parents):
    length = parents.shape[-1]
    column = jnp.arange(length, dtype=jnp.int32)
    reached = (parents[..., :, None] == column).astype(jnp.float32) + jnp.eye(
        length, dtype=jnp.float32
    )
    for repeat in range(max(1, (length - 1).bit_length())):
        reached = (jnp.einsum("...ij,...jk->...ik", reached, reached, precision=HIGH) > 0.5).astype(
            jnp.float32
        )
    return reached > 0.5


def slot_numbers(picked_ids):
    flattened = picked_ids.reshape(-1)
    onehot = (flattened[:, None] == jnp.arange(EXPERTS, dtype=jnp.int32)[None, :]).astype(jnp.int32)
    before = jnp.cumsum(onehot, axis=0) - onehot
    return jnp.sum(before * onehot, axis=1).reshape(picked_ids.shape)


SCALE = HDIM ** (-0.5)
NT = (((1,), (1,)), ((), ()))


def head_masks(rows):
    head = lax.broadcasted_iota(jnp.int32, (rows, LANES), 1) // HDIM
    return [(head == h).astype(jnp.float32).astype(jnp.bfloat16) for h in range(PACK)]


def local_kernel(len_ref, q_ref, kc_ref, vc_ref, kd_ref, vd_ref, anc_ref, acc_ref, stat_ref):
    b, g = pl.program_id(0), pl.program_id(1)
    tree = q_ref.shape[1]
    q = q_ref[0]
    masks = head_masks(tree)
    stacked = jnp.concatenate([q * mask for mask in masks], axis=0)
    s_cache = lax.dot_general(stacked, kc_ref[0], NT, preferred_element_type=jnp.float32) * SCALE
    slot = lax.broadcasted_iota(jnp.int32, s_cache.shape, 1)
    s_cache = jnp.where(slot < len_ref[b], s_cache, -jnp.inf)
    s_tree = lax.dot_general(stacked, kd_ref[0], NT, preferred_element_type=jnp.float32) * SCALE
    anc = jnp.concatenate([anc_ref[0]] * PACK, axis=0)
    s_tree = jnp.where(anc > 0.5, s_tree, -jnp.inf)
    top = jnp.maximum(
        jnp.max(s_cache, axis=1, keepdims=True), jnp.max(s_tree, axis=1, keepdims=True)
    )
    w_cache = jnp.exp(s_cache - top)
    w_tree = jnp.exp(s_tree - top)
    total = jnp.sum(w_cache, axis=1, keepdims=True) + jnp.sum(w_tree, axis=1, keepdims=True)
    mixed = jnp.dot(w_cache.astype(jnp.bfloat16), vc_ref[0], preferred_element_type=jnp.float32)
    mixed += jnp.dot(w_tree.astype(jnp.bfloat16), vd_ref[0], preferred_element_type=jnp.float32)
    head = lax.broadcasted_iota(jnp.int32, (tree, LANES), 1) // HDIM
    lane = lax.broadcasted_iota(jnp.int32, (tree, STAT), 1)

    @pl.when(g == 0)
    def _():
        stat_ref[...] = jnp.zeros_like(stat_ref)

    out = jnp.zeros((tree, LANES), jnp.float32)
    stat = stat_ref[0]
    for h in range(PACK):
        rows = slice(h * tree, (h + 1) * tree)
        out = jnp.where(head == h, mixed[rows], out)
        stat = jnp.where(lane == g * PACK + h, top[rows], stat)
        stat = jnp.where(lane == STAT // 2 + g * PACK + h, total[rows], stat)
    acc_ref[0] = out
    stat_ref[0] = stat


def prompt_kernel(q_ref, group_ref, k_ref, v_ref, acc_ref, stat_ref):
    g = pl.program_id(0)
    sources, rows = q_ref.shape[0], q_ref.shape[1]
    groups, positions = k_ref.shape[0], k_ref.shape[1]
    keys = groups * positions
    k = k_ref[...].reshape(keys, LANES)
    v = v_ref[...].reshape(keys, LANES)
    masks = head_masks(keys)
    k_wide = jnp.concatenate([k * mask for mask in masks], axis=0)
    v_wide = jnp.concatenate([v * mask for mask in masks], axis=0)
    key_group = (lax.broadcasted_iota(jnp.int32, (rows, keys), 1) // positions).astype(jnp.float32)
    lane = lax.broadcasted_iota(jnp.int32, (rows, STAT), 1)

    @pl.when(g == 0)
    def _():
        stat_ref[...] = jnp.zeros_like(stat_ref)

    for s in range(sources):
        scores = lax.dot_general(q_ref[s], k_wide, NT, preferred_element_type=jnp.float32) * SCALE
        live = key_group == group_ref[s].astype(jnp.float32)[:, :1]
        stat = stat_ref[s]
        weights = []
        for h in range(PACK):
            part = jnp.where(live, scores[:, h * keys : (h + 1) * keys], -jnp.inf)
            top = jnp.max(part, axis=1, keepdims=True)
            weight = jnp.exp(part - top)
            stat = jnp.where(lane == g * PACK + h, top, stat)
            stat = jnp.where(
                lane == STAT // 2 + g * PACK + h, jnp.sum(weight, axis=1, keepdims=True), stat
            )
            weights.append(weight.astype(jnp.bfloat16))
        stat_ref[s] = stat
        acc_ref[s] = jnp.dot(
            jnp.concatenate(weights, axis=1), v_wide, preferred_element_type=jnp.float32
        ).astype(jnp.bfloat16)


def merge_kernel(
    part_ref, pstat_ref, acc_ref, stat_ref, residual_ref, gain_ref, att_ref, stream_ref, normed_ref
):
    sources, rows, width = part_ref.shape
    stats = [stat_ref[...]] + [pstat_ref[s] for s in range(sources)]
    top = stats[0]
    for stat in stats[1:]:
        top = jnp.maximum(top, stat)
    scales = [jnp.exp(stat - top) for stat in stats]
    total = sum(scale * pltpu.roll(stat, STAT // 2, 1) for scale, stat in zip(scales, stats))
    scales = [scale / total for scale in scales]
    squares = jnp.zeros((rows, 1), jnp.float32)
    left = lax.broadcasted_iota(jnp.int32, (rows, STAT), 1) < HDIM
    for pair in range(width // STAT):
        cols = slice(pair * STAT, (pair + 1) * STAT)
        a = 2 * pair
        out = jnp.zeros((rows, STAT), jnp.float32)
        for i in range(sources + 1):
            values = acc_ref[:, cols] if i == 0 else part_ref[i - 1, :, cols].astype(jnp.float32)
            out += values * jnp.where(left, scales[i][:, a : a + 1], scales[i][:, a + 1 : a + 2])
        attended = out.astype(jnp.bfloat16)
        att_ref[:, cols] = attended
        stream = (
            residual_ref[:, cols].astype(jnp.float32) + attended.astype(jnp.float32)
        ).astype(jnp.bfloat16)
        stream_ref[:, cols] = stream
        stream = stream.astype(jnp.float32)
        squares += jnp.sum(stream * stream, axis=1, keepdims=True)
    factor = lax.rsqrt(squares / width + EPSILON)
    normed_ref[...] = (
        stream_ref[...].astype(jnp.float32) * factor * gain_ref[...]
    ).astype(jnp.bfloat16)


def attention(
    queries, draft_keys, draft_values, tree_parents, cache_keys, cache_values, cache_lengths,
    prompt_keys, prompt_values, group_ids, residual, norm_gain,
):
    requests, tree, width = queries.shape
    rows, packs, cache = requests * tree, width // LANES, cache_keys.shape[1]
    groups, positions = prompt_keys.shape[:2]
    row_group = jnp.broadcast_to(
        jnp.repeat(group_ids, tree)[:, None].astype(jnp.bfloat16), (rows, STAT)
    )
    sent = jnp.concatenate([queries.reshape(rows, width), row_group], axis=1)
    plane = lax.all_gather(sent, "exp", axis=0, tiled=False)
    sources = plane.shape[0]
    anc = ancestry(tree_parents).astype(jnp.float32)
    block = lambda n: pl.BlockSpec((1, n, LANES), lambda b, g, _: (b, 0, g))
    flops = 4 * rows * PACK * width * (cache + tree)
    acc, stat = pl.pallas_call(
        local_kernel,
        grid_spec=pltpu.PrefetchScalarGridSpec(
            num_scalar_prefetch=1,
            grid=(requests, packs),
            in_specs=[
                block(tree), block(cache), block(cache), block(tree), block(tree),
                pl.BlockSpec((1, tree, tree), lambda b, g, _: (b, 0, 0)),
            ],
            out_specs=[block(tree), pl.BlockSpec((1, tree, STAT), lambda b, g, _: (b, 0, 0))],
        ),
        out_shape=[
            jax.ShapeDtypeStruct((requests, tree, width), jnp.float32),
            jax.ShapeDtypeStruct((requests, tree, STAT), jnp.float32),
        ],
        cost_estimate=pl.CostEstimate(
            flops=flops, bytes_accessed=4 * requests * cache * width,
            transcendentals=rows * HEADS * cache,
        ),
        name="local_attention",
    )(cache_lengths, queries, cache_keys, cache_values, draft_keys, draft_values, anc)
    pblock = pl.BlockSpec((groups, positions, LANES), lambda g: (0, 0, g))
    part, pstat = pl.pallas_call(
        prompt_kernel,
        grid=(packs,),
        in_specs=[
            pl.BlockSpec((sources, rows, LANES), lambda g: (0, 0, g)),
            pl.BlockSpec((sources, rows, STAT), lambda g: (0, 0, width // STAT)),
            pblock,
            pblock,
        ],
        out_specs=[
            pl.BlockSpec((sources, rows, LANES), lambda g: (0, 0, g)),
            pl.BlockSpec((sources, rows, STAT), lambda g: (0, 0, 0)),
        ],
        out_shape=[
            jax.ShapeDtypeStruct((sources, rows, width), jnp.bfloat16),
            jax.ShapeDtypeStruct((sources, rows, STAT), jnp.float32),
        ],
        name="prompt_attention",
    )(plane, plane, prompt_keys, prompt_values)
    part = lax.all_to_all(part, "exp", split_axis=0, concat_axis=0, tiled=True)
    pstat = lax.all_to_all(pstat, "exp", split_axis=0, concat_axis=0, tiled=True)
    return pl.pallas_call(
        merge_kernel,
        out_shape=[jax.ShapeDtypeStruct((rows, width), jnp.bfloat16)] * 3,
        compiler_params=pltpu.CompilerParams(vmem_limit_bytes=32 * 1024 * 1024),
        name="merge",
    )(
        part, pstat, acc.reshape(rows, width), stat.reshape(rows, STAT),
        residual.reshape(rows, width), norm_gain.reshape(1, width),
    )


def greet(peers):
    barrier = pltpu.get_barrier_semaphore()
    for axis, size in peers:
        me = lax.axis_index(axis)
        for step in range(1, size):
            pl.semaphore_signal(
                barrier, inc=1, device_id={axis: lax.rem(me + step, size)},
                device_id_type=pl.DeviceIdType.MESH,
            )
    pl.semaphore_wait(barrier, sum(size - 1 for _, size in peers))


def remote(src, dst, send, recv, axis, target):
    return pltpu.make_async_remote_copy(
        src_ref=src, dst_ref=dst, send_sem=send, recv_sem=recv, device_id={axis: target},
        device_id_type=pl.DeviceIdType.MESH,
    )


def dispatch_kernel(
    depth, size, rows_ref, pick_ref, out_ref, held, staged, zsend, zrecv, psend, precv, own
):
    z, e = lax.axis_index("req"), lax.axis_index("exp")
    experts, cap = pick_ref.shape[1], pick_ref.shape[2]
    holders = size // experts
    greet((("req", depth), ("exp", size)))
    along = []
    for k in range(1, depth):
        copy = remote(
            rows_ref, held.at[k - 1], zsend.at[k - 1], zrecv.at[k - 1], "req",
            lax.rem(z + k, depth),
        )
        copy.start()
        along.append(copy)
    started, locals_ = [], []
    for k in range(depth):
        source = lax.rem(z - k + depth, depth)
        if k:
            along[k - 1].wait_recv()
        rows = rows_ref[...] if k == 0 else held[k - 1]
        for x in range(experts):
            staged[k, x] = jnp.dot(
                pick_ref[source, x], rows, preferred_element_type=jnp.float32
            ).astype(jnp.bfloat16)
        for o in range(1, size):
            target = lax.rem(e + o, size)
            copy = remote(
                staged.at[k, target // holders], out_ref.at[source, e], psend.at[k, o - 1],
                precv.at[k, o - 1], "exp", target,
            )
            copy.start()
            started.append((copy, k, o, source))
        copy = pltpu.make_async_copy(staged.at[k, e // holders], out_ref.at[source, e], own.at[k])
        copy.start()
        locals_.append(copy)
    for copy in along:
        copy.wait_send()
    for copy in locals_:
        copy.wait()
    for copy, k, o, source in started:
        copy.wait_send()
        origin = lax.rem(e - o + size, size)
        remote(
            staged.at[k, 0], out_ref.at[source, origin], psend.at[k, o - 1], precv.at[k, o - 1],
            "exp", origin,
        ).wait_recv()


def collect_kernel(
    depth, size, y_ref, mix_ref, stream_ref, out_ref, landed, partial, held,
    zsend, zrecv, psend, precv, own,
):
    z, e = lax.axis_index("req"), lax.axis_index("exp")
    experts = mix_ref.shape[1]
    rows = stream_ref.shape[0]
    holders = size // experts
    greet((("req", depth), ("exp", size)))
    started = []
    order = list(range(1, depth)) + [0]
    for k in order:
        home = lax.rem(z + k, depth)
        group = []
        for o in range(1, size):
            target = lax.rem(e + o, size)
            copy = remote(
                y_ref.at[home, target], landed.at[k, e], psend.at[k, o - 1], precv.at[k, o - 1],
                "exp", target,
            )
            copy.start()
            group.append(copy)
        copy = pltpu.make_async_copy(y_ref.at[home, e], landed.at[k, e], own.at[k])
        copy.start()
        started.append((k, home, group, copy))
    along = []
    for k, home, group, mine in started:
        mine.wait()
        for o in range(1, size):
            origin = lax.rem(e - o + size, size)
            remote(
                y_ref.at[home, origin], landed.at[k, origin], psend.at[k, o - 1],
                precv.at[k, o - 1], "exp", origin,
            ).wait_recv()
        total = None
        for s in range(size):
            both = jnp.dot(
                mix_ref[home, s // holders], landed[k, s], preferred_element_type=jnp.float32
            )
            total = both if total is None else total + both
        total = total[:rows] + total[rows:]
        if k == 0:
            kept = total + stream_ref[...].astype(jnp.float32)
        else:
            partial[k - 1] = total.astype(jnp.bfloat16)
            copy = remote(
                partial.at[k - 1], held.at[k - 1], zsend.at[k - 1], zrecv.at[k - 1], "req", home
            )
            copy.start()
            along.append(copy)
    for i, copy in enumerate(along):
        copy.wait_recv()
        kept += held[i].astype(jnp.float32)
    out_ref[...] = kept.astype(jnp.bfloat16)
    for copy in along:
        copy.wait_send()
    for _, _, group, _ in started:
        for copy in group:
            copy.wait_send()


def dispatch(normed, pick, depth, size):
    rows, width = normed.shape
    cap = pick.shape[2]
    dma = pltpu.SemaphoreType.DMA
    vmem = pl.BlockSpec(memory_space=pltpu.VMEM)
    return pl.pallas_call(
        functools.partial(dispatch_kernel, depth, size),
        out_shape=jax.ShapeDtypeStruct((depth, size, cap, width), jnp.bfloat16),
        in_specs=[vmem, vmem],
        out_specs=pl.BlockSpec(memory_space=pl.ANY),
        scratch_shapes=[
            pltpu.VMEM((depth - 1, rows, width), jnp.bfloat16),
            pltpu.VMEM((depth, pick.shape[1], cap, width), jnp.bfloat16),
            dma((depth - 1,)), dma((depth - 1,)),
            dma((depth, size - 1)), dma((depth, size - 1)), dma((depth,)),
        ],
        compiler_params=pltpu.CompilerParams(
            collective_id=0, has_side_effects=True, vmem_limit_bytes=40 * 1024 * 1024
        ),
        name="dispatch",
    )(normed, pick)


def collect(y, mix, stream, depth, size):
    rows, width = stream.shape
    cap = y.shape[2]
    dma = pltpu.SemaphoreType.DMA
    vmem = pl.BlockSpec(memory_space=pltpu.VMEM)
    return pl.pallas_call(
        functools.partial(collect_kernel, depth, size),
        out_shape=jax.ShapeDtypeStruct((rows, width), jnp.bfloat16),
        in_specs=[pl.BlockSpec(memory_space=pl.ANY), vmem, vmem],
        out_specs=vmem,
        scratch_shapes=[
            pltpu.VMEM((depth, size, cap, width), jnp.bfloat16),
            pltpu.VMEM((depth - 1, rows, width), jnp.bfloat16),
            pltpu.VMEM((depth - 1, rows, width), jnp.bfloat16),
            dma((depth - 1,)), dma((depth - 1,)),
            dma((depth, size - 1)), dma((depth, size - 1)), dma((depth,)),
        ],
        compiler_params=pltpu.CompilerParams(
            collective_id=1, has_side_effects=True, vmem_limit_bytes=48 * 1024 * 1024
        ),
        name="collect",
    )(y, mix, stream)


def on_device(
    queries,
    draft_keys,
    draft_values,
    tree_parents,
    cache_keys,
    cache_values,
    cache_lengths,
    prompt_keys,
    prompt_values,
    group_ids,
    residual,
    norm_gain,
    router,
    w_gate,
    w_up,
    w_down,
    expert_ids,
    accepted_rows,
):
    requests, tree_len, width = queries.shape
    row_count = requests * tree_len
    attended, stream, normed = attention(
        queries, draft_keys, draft_values, tree_parents, cache_keys, cache_values, cache_lengths,
        prompt_keys, prompt_values, group_ids, residual, norm_gain,
    )
    attended = attended.reshape(requests, tree_len, width)
    logits = jnp.dot(normed, router, preferred_element_type=jnp.float32)
    routed = expert_ids.reshape(row_count, TOPK)
    chosen = jnp.take_along_axis(logits, routed, axis=1)
    gate_first = 1.0 / (1.0 + jnp.exp(chosen[:, 1] - chosen[:, 0]))
    gates = jnp.stack([gate_first, 1.0 - gate_first], axis=1)
    depth, size = lax.axis_size("req"), lax.axis_size("exp")
    all_routed = lax.all_gather(routed, "req", axis=0, tiled=False)
    all_gates = lax.all_gather(gates, "req", axis=0, tiled=False)
    target = all_routed * CAP + jax.vmap(slot_numbers)(all_routed)
    slots = jnp.arange(EXPERTS * CAP, dtype=jnp.int32).reshape(EXPERTS, CAP)
    pick = (target[:, None, None, :, 0] == slots[None, :, :, None]) | (
        target[:, None, None, :, 1] == slots[None, :, :, None]
    )
    pick = pick.astype(jnp.bfloat16)
    hit = target[:, None, :, None, :] == slots[None, :, None, :, None]
    mix = jnp.sum(jnp.where(hit, all_gates[:, None, :, None, :], 0.0), axis=-1)
    mix_high = mix.astype(jnp.bfloat16)
    mix_low = (mix - lax.reduce_precision(mix, 8, 7)).astype(jnp.bfloat16)
    mix = jnp.concatenate([mix_high, mix_low], axis=2)
    arrived = dispatch(normed, pick, depth, size)
    row_piece = arrived.reshape(-1, width)
    gate_proj = jnp.dot(row_piece, w_gate[0], preferred_element_type=jnp.float32)
    up_proj = jnp.dot(row_piece, w_up[0], preferred_element_type=jnp.float32)
    hidden = (jax.nn.silu(gate_proj) * up_proj).astype(jnp.bfloat16)
    pieces = jnp.dot(hidden, w_down[0], preferred_element_type=jnp.float32).astype(jnp.bfloat16)
    layer_out = collect(
        pieces.reshape(depth, size, CAP, width), mix, stream, depth, size
    ).reshape(requests, tree_len, width)
    kept_keys = jnp.take_along_axis(draft_keys, accepted_rows[:, :, None], axis=1)
    kept_values = jnp.take_along_axis(draft_values, accepted_rows[:, :, None], axis=1)
    accepted_cache = jnp.stack([kept_keys, kept_values], axis=1)
    return (attended, layer_out, accepted_cache)


def solution(mesh):
    return jax.shard_map(
        on_device,
        mesh=mesh,
        in_specs=(
            P(("req", "exp"), None, None),
            P(("req", "exp"), None, None),
            P(("req", "exp"), None, None),
            P(("req", "exp"), None),
            P(("req", "exp"), None, None),
            P(("req", "exp"), None, None),
            P(("req", "exp")),
            P("req", "exp", None),
            P("req", "exp", None),
            P(("req", "exp")),
            P(("req", "exp"), None, None),
            P(),
            P(),
            P("exp", None, "req"),
            P("exp", None, "req"),
            P("exp", "req", None),
            P(("req", "exp"), None, None),
            P(("req", "exp"), None),
        ),
        out_specs=(
            P(("req", "exp"), None, None),
            P(("req", "exp"), None, None),
            P(("req", "exp"), None, None, None),
        ),
        check_vma=False,
    )
```

```python
import functools

import jax
import jax.numpy as jnp
from jax import lax
from jax.experimental import pallas as pl
from jax.experimental.pallas import tpu as pltpu
from jax.sharding import PartitionSpec as P

HEADS = 36
HDIM = 64
EXPERTS = 8
TOPK = 2
GRP = 2
CAP = 18
LANES = 256
PACK = LANES // HDIM
STAT = 128


HIGH = lax.Precision.HIGHEST
EPSILON = 1e-05


def ancestry(parents):
    length = parents.shape[-1]
    column = jnp.arange(length, dtype=jnp.int32)
    reached = (parents[..., :, None] == column).astype(jnp.float32) + jnp.eye(
        length, dtype=jnp.float32
    )
    for repeat in range(max(1, (length - 1).bit_length())):
        reached = (jnp.einsum("...ij,...jk->...ik", reached, reached, precision=HIGH) > 0.5).astype(
            jnp.float32
        )
    return reached > 0.5


def slot_numbers(picked_ids):
    flattened = picked_ids.reshape(-1)
    onehot = (flattened[:, None] == jnp.arange(EXPERTS, dtype=jnp.int32)[None, :]).astype(jnp.int32)
    before = jnp.cumsum(onehot, axis=0) - onehot
    return jnp.sum(before * onehot, axis=1).reshape(picked_ids.shape)


SCALE = HDIM ** (-0.5)
NT = (((1,), (1,)), ((), ()))


def head_masks(rows):
    head = lax.broadcasted_iota(jnp.int32, (rows, LANES), 1) // HDIM
    return [(head == h).astype(jnp.float32).astype(jnp.bfloat16) for h in range(PACK)]


def local_kernel(len_ref, q_ref, kc_ref, vc_ref, kd_ref, vd_ref, anc_ref, acc_ref, stat_ref):
    b, g = pl.program_id(0), pl.program_id(1)
    tree = q_ref.shape[1]
    q = q_ref[0]
    masks = head_masks(tree)
    stacked = jnp.concatenate([q * mask for mask in masks], axis=0)
    s_cache = lax.dot_general(stacked, kc_ref[0], NT, preferred_element_type=jnp.float32) * SCALE
    slot = lax.broadcasted_iota(jnp.int32, s_cache.shape, 1)
    s_cache = jnp.where(slot < len_ref[b], s_cache, -jnp.inf)
    s_tree = lax.dot_general(stacked, kd_ref[0], NT, preferred_element_type=jnp.float32) * SCALE
    anc = jnp.concatenate([anc_ref[0]] * PACK, axis=0)
    s_tree = jnp.where(anc > 0.5, s_tree, -jnp.inf)
    top = jnp.maximum(
        jnp.max(s_cache, axis=1, keepdims=True), jnp.max(s_tree, axis=1, keepdims=True)
    )
    w_cache = jnp.exp(s_cache - top)
    w_tree = jnp.exp(s_tree - top)
    total = jnp.sum(w_cache, axis=1, keepdims=True) + jnp.sum(w_tree, axis=1, keepdims=True)
    mixed = jnp.dot(w_cache.astype(jnp.bfloat16), vc_ref[0], preferred_element_type=jnp.float32)
    mixed += jnp.dot(w_tree.astype(jnp.bfloat16), vd_ref[0], preferred_element_type=jnp.float32)
    head = lax.broadcasted_iota(jnp.int32, (tree, LANES), 1) // HDIM
    lane = lax.broadcasted_iota(jnp.int32, (tree, STAT), 1)

    @pl.when(g == 0)
    def _():
        stat_ref[...] = jnp.zeros_like(stat_ref)

    out = jnp.zeros((tree, LANES), jnp.float32)
    stat = stat_ref[0]
    for h in range(PACK):
        rows = slice(h * tree, (h + 1) * tree)
        out = jnp.where(head == h, mixed[rows], out)
        stat = jnp.where(lane == g * PACK + h, top[rows], stat)
        stat = jnp.where(lane == STAT // 2 + g * PACK + h, total[rows], stat)
    acc_ref[0] = out
    stat_ref[0] = stat


def prompt_kernel(
    size, plane_ref, k_ref, v_ref, acc_ref, stat_ref, residual_ref, gain_ref,
    att_ref, stream_ref, normed_ref,
    k_wide, v_wide, staged, sstat, landed, lstat, asend, arecv, ssend, srecv,
):
    me = lax.axis_index("exp")
    rows, width = acc_ref.shape
    groups, positions = k_ref.shape[0], k_ref.shape[1]
    keys, packs = groups * positions, width // LANES
    masks = head_masks(keys)
    greet((("exp", size),))

    def columns(g):
        return pl.ds(pl.multiple_of(g * LANES, LANES), LANES)

    def widen(g, carry):
        k = k_ref[:, :, columns(g)].reshape(keys, LANES)
        v = v_ref[:, :, columns(g)].reshape(keys, LANES)
        for h in range(PACK):
            k_wide[g, h * keys : (h + 1) * keys] = k * masks[h]
            v_wide[g, h * keys : (h + 1) * keys] = v * masks[h]
        return carry

    lax.fori_loop(0, packs, widen, 0)
    key_group = (lax.broadcasted_iota(jnp.int32, (rows, keys), 1) // positions).astype(jnp.float32)
    lane = lax.broadcasted_iota(jnp.int32, (rows, STAT), 1)
    copies = []
    for o in list(range(1, size)) + [0]:
        source = lax.rem(me + o, size)
        live = key_group == plane_ref[source, :, width : width + STAT].astype(jnp.float32)[:, :1]
        target, tstat = (staged.at[o - 1], sstat.at[o - 1]) if o else (landed.at[me], lstat.at[me])

        def attend(g, stat):
            scores = lax.dot_general(
                plane_ref[source, :, columns(g)], k_wide[g], NT,
                preferred_element_type=jnp.float32,
            ) * SCALE
            weights = []
            for h in range(PACK):
                part = jnp.where(live, scores[:, h * keys : (h + 1) * keys], -jnp.inf)
                top = jnp.max(part, axis=1, keepdims=True)
                weight = jnp.exp(part - top)
                total = jnp.sum(weight, axis=1, keepdims=True)
                stat = jnp.where(lane == g * PACK + h, top, stat)
                stat = jnp.where(lane == STAT // 2 + g * PACK + h, total, stat)
                weights.append(weight.astype(jnp.bfloat16))
            target[:, columns(g)] = jnp.dot(
                jnp.concatenate(weights, axis=1), v_wide[g], preferred_element_type=jnp.float32
            ).astype(jnp.bfloat16)
            return stat

        tstat[...] = lax.fori_loop(0, packs, attend, jnp.zeros((rows, STAT), jnp.float32))
        if o:
            for copy in (
                remote(target, landed.at[me], asend.at[o - 1], arecv.at[o - 1], "exp", source),
                remote(tstat, lstat.at[me], ssend.at[o - 1], srecv.at[o - 1], "exp", source),
            ):
                copy.start()
                copies.append(copy)
    for copy in copies:
        copy.wait_send()
    for o in range(1, size):
        origin = lax.rem(me - o + size, size)
        remote(
            staged.at[o - 1], landed.at[origin], asend.at[o - 1], arecv.at[o - 1], "exp", origin
        ).wait_recv()
        remote(
            sstat.at[o - 1], lstat.at[origin], ssend.at[o - 1], srecv.at[o - 1], "exp", origin
        ).wait_recv()
    merge_kernel(
        landed, lstat, acc_ref, stat_ref, residual_ref, gain_ref, att_ref, stream_ref, normed_ref
    )


def merge_kernel(
    part_ref, pstat_ref, acc_ref, stat_ref, residual_ref, gain_ref, att_ref, stream_ref, normed_ref
):
    sources, rows, width = part_ref.shape
    stats = [stat_ref[...]] + [pstat_ref[s] for s in range(sources)]
    top = stats[0]
    for stat in stats[1:]:
        top = jnp.maximum(top, stat)
    scales = [jnp.exp(stat - top) for stat in stats]
    total = sum(scale * pltpu.roll(stat, STAT // 2, 1) for scale, stat in zip(scales, stats))
    scales = [scale / total for scale in scales]
    squares = jnp.zeros((rows, 1), jnp.float32)
    left = lax.broadcasted_iota(jnp.int32, (rows, STAT), 1) < HDIM
    for pair in range(width // STAT):
        cols = slice(pair * STAT, (pair + 1) * STAT)
        a = 2 * pair
        out = jnp.zeros((rows, STAT), jnp.float32)
        for i in range(sources + 1):
            values = acc_ref[:, cols] if i == 0 else part_ref[i - 1, :, cols].astype(jnp.float32)
            out += values * jnp.where(left, scales[i][:, a : a + 1], scales[i][:, a + 1 : a + 2])
        attended = out.astype(jnp.bfloat16)
        att_ref[:, cols] = attended
        stream = (
            residual_ref[:, cols].astype(jnp.float32) + attended.astype(jnp.float32)
        ).astype(jnp.bfloat16)
        stream_ref[:, cols] = stream
        stream = stream.astype(jnp.float32)
        squares += jnp.sum(stream * stream, axis=1, keepdims=True)
    factor = lax.rsqrt(squares / width + EPSILON)
    normed_ref[...] = (
        stream_ref[...].astype(jnp.float32) * factor * gain_ref[...]
    ).astype(jnp.bfloat16)


def attention(
    queries, draft_keys, draft_values, tree_parents, cache_keys, cache_values, cache_lengths,
    prompt_keys, prompt_values, group_ids, residual, norm_gain,
):
    requests, tree, width = queries.shape
    rows, packs, cache = requests * tree, width // LANES, cache_keys.shape[1]
    groups, positions = prompt_keys.shape[:2]
    row_group = jnp.broadcast_to(
        jnp.repeat(group_ids, tree)[:, None].astype(jnp.bfloat16), (rows, STAT)
    )
    sent = jnp.concatenate([queries.reshape(rows, width), row_group], axis=1)
    plane = lax.all_gather(sent, "exp", axis=0, tiled=False)
    sources = plane.shape[0]
    anc = ancestry(tree_parents).astype(jnp.float32)
    block = lambda n: pl.BlockSpec((1, n, LANES), lambda b, g, _: (b, 0, g))
    flops = 4 * rows * PACK * width * (cache + tree)
    acc, stat = pl.pallas_call(
        local_kernel,
        grid_spec=pltpu.PrefetchScalarGridSpec(
            num_scalar_prefetch=1,
            grid=(requests, packs),
            in_specs=[
                block(tree), block(cache), block(cache), block(tree), block(tree),
                pl.BlockSpec((1, tree, tree), lambda b, g, _: (b, 0, 0)),
            ],
            out_specs=[block(tree), pl.BlockSpec((1, tree, STAT), lambda b, g, _: (b, 0, 0))],
        ),
        out_shape=[
            jax.ShapeDtypeStruct((requests, tree, width), jnp.float32),
            jax.ShapeDtypeStruct((requests, tree, STAT), jnp.float32),
        ],
        cost_estimate=pl.CostEstimate(
            flops=flops, bytes_accessed=4 * requests * cache * width,
            transcendentals=rows * HEADS * cache,
        ),
        name="local_attention",
    )(cache_lengths, queries, cache_keys, cache_values, draft_keys, draft_values, anc)
    keys = groups * positions
    vmem = pl.BlockSpec(memory_space=pltpu.VMEM)
    dma = pltpu.SemaphoreType.DMA
    return pl.pallas_call(
        functools.partial(prompt_kernel, sources),
        out_shape=[jax.ShapeDtypeStruct((rows, width), jnp.bfloat16)] * 3,
        in_specs=[vmem] * 7,
        out_specs=[vmem] * 3,
        scratch_shapes=[
            pltpu.VMEM((packs, PACK * keys, LANES), jnp.bfloat16),
            pltpu.VMEM((packs, PACK * keys, LANES), jnp.bfloat16),
            pltpu.VMEM((sources - 1, rows, width), jnp.bfloat16),
            pltpu.VMEM((sources - 1, rows, STAT), jnp.float32),
            pltpu.VMEM((sources, rows, width), jnp.bfloat16),
            pltpu.VMEM((sources, rows, STAT), jnp.float32),
            dma((sources - 1,)), dma((sources - 1,)), dma((sources - 1,)), dma((sources - 1,)),
        ],
        compiler_params=pltpu.CompilerParams(
            collective_id=2, has_side_effects=True, vmem_limit_bytes=48 * 1024 * 1024
        ),
        name="prompt_attention",
    )(
        plane, prompt_keys, prompt_values, acc.reshape(rows, width), stat.reshape(rows, STAT),
        residual.reshape(rows, width), norm_gain.reshape(1, width),
    )


def greet(peers):
    barrier = pltpu.get_barrier_semaphore()
    for axis, size in peers:
        me = lax.axis_index(axis)
        for step in range(1, size):
            pl.semaphore_signal(
                barrier, inc=1, device_id={axis: lax.rem(me + step, size)},
                device_id_type=pl.DeviceIdType.MESH,
            )
    pl.semaphore_wait(barrier, sum(size - 1 for _, size in peers))


def remote(src, dst, send, recv, axis, target):
    return pltpu.make_async_remote_copy(
        src_ref=src, dst_ref=dst, send_sem=send, recv_sem=recv, device_id={axis: target},
        device_id_type=pl.DeviceIdType.MESH,
    )


def dispatch_kernel(
    depth, size, rows_ref, pick_ref, router_ref, out_ref, logits_ref, held, staged, zsend, zrecv, psend, precv, own
):
    z, e = lax.axis_index("req"), lax.axis_index("exp")
    experts, cap = pick_ref.shape[1], pick_ref.shape[2]
    holders = size // experts
    greet((("req", depth), ("exp", size)))
    along = []
    for k in range(1, depth):
        copy = remote(
            rows_ref, held.at[k - 1], zsend.at[k - 1], zrecv.at[k - 1], "req",
            lax.rem(z + k, depth),
        )
        copy.start()
        along.append(copy)
    started, locals_ = [], []
    for k in range(depth):
        source = lax.rem(z - k + depth, depth)
        if k:
            along[k - 1].wait_recv()
        rows = rows_ref[...] if k == 0 else held[k - 1]
        for x in range(experts):
            staged[k, x] = jnp.dot(
                pick_ref[source, x], rows, preferred_element_type=jnp.float32
            ).astype(jnp.bfloat16)
        logits_ref[source] = jnp.dot(rows, router_ref[...], preferred_element_type=jnp.float32)
        for o in range(1, size):
            target = lax.rem(e + o, size)
            copy = remote(
                staged.at[k, target // holders], out_ref.at[source, e], psend.at[k, o - 1],
                precv.at[k, o - 1], "exp", target,
            )
            copy.start()
            started.append((copy, k, o, source))
        copy = pltpu.make_async_copy(staged.at[k, e // holders], out_ref.at[source, e], own.at[k])
        copy.start()
        locals_.append(copy)
    for copy in along:
        copy.wait_send()
    for copy in locals_:
        copy.wait()
    for copy, k, o, source in started:
        copy.wait_send()
        origin = lax.rem(e - o + size, size)
        remote(
            staged.at[k, 0], out_ref.at[source, origin], psend.at[k, o - 1], precv.at[k, o - 1],
            "exp", origin,
        ).wait_recv()


def collect_kernel(
    depth, size, y_ref, mix_ref, stream_ref, out_ref, landed, partial, held,
    zsend, zrecv, psend, precv, own,
):
    z, e = lax.axis_index("req"), lax.axis_index("exp")
    experts = mix_ref.shape[1]
    rows = stream_ref.shape[0]
    holders = size // experts
    greet((("req", depth), ("exp", size)))
    started = []
    order = list(range(1, depth)) + [0]
    for k in order:
        home = lax.rem(z + k, depth)
        group = []
        for o in range(1, size):
            target = lax.rem(e + o, size)
            copy = remote(
                y_ref.at[home, target], landed.at[k, e], psend.at[k, o - 1], precv.at[k, o - 1],
                "exp", target,
            )
            copy.start()
            group.append(copy)
        copy = pltpu.make_async_copy(y_ref.at[home, e], landed.at[k, e], own.at[k])
        copy.start()
        started.append((k, home, group, copy))
    along = []
    for k, home, group, mine in started:
        mine.wait()
        for o in range(1, size):
            origin = lax.rem(e - o + size, size)
            remote(
                y_ref.at[home, origin], landed.at[k, origin], psend.at[k, o - 1],
                precv.at[k, o - 1], "exp", origin,
            ).wait_recv()
        total = None
        for s in range(size):
            both = jnp.dot(
                mix_ref[home, s // holders], landed[k, s], preferred_element_type=jnp.float32
            )
            total = both if total is None else total + both
        total = total[:rows] + total[rows:]
        if k == 0:
            kept = total + stream_ref[...].astype(jnp.float32)
        else:
            partial[k - 1] = total.astype(jnp.bfloat16)
            copy = remote(
                partial.at[k - 1], held.at[k - 1], zsend.at[k - 1], zrecv.at[k - 1], "req", home
            )
            copy.start()
            along.append(copy)
    for i, copy in enumerate(along):
        copy.wait_recv()
        kept += held[i].astype(jnp.float32)
    out_ref[...] = kept.astype(jnp.bfloat16)
    for copy in along:
        copy.wait_send()
    for _, _, group, _ in started:
        for copy in group:
            copy.wait_send()


def dispatch(normed, pick, router, depth, size):
    rows, width = normed.shape
    cap = pick.shape[2]
    dma = pltpu.SemaphoreType.DMA
    vmem = pl.BlockSpec(memory_space=pltpu.VMEM)
    return pl.pallas_call(
        functools.partial(dispatch_kernel, depth, size),
        out_shape=[
            jax.ShapeDtypeStruct((depth, size, cap, width), jnp.bfloat16),
            jax.ShapeDtypeStruct((depth, rows, STAT), jnp.float32),
        ],
        in_specs=[vmem, vmem, vmem],
        out_specs=[pl.BlockSpec(memory_space=pl.ANY), vmem],
        scratch_shapes=[
            pltpu.VMEM((depth - 1, rows, width), jnp.bfloat16),
            pltpu.VMEM((depth, pick.shape[1], cap, width), jnp.bfloat16),
            dma((depth - 1,)), dma((depth - 1,)),
            dma((depth, size - 1)), dma((depth, size - 1)), dma((depth,)),
        ],
        compiler_params=pltpu.CompilerParams(
            collective_id=0, has_side_effects=True, vmem_limit_bytes=40 * 1024 * 1024
        ),
        name="dispatch",
    )(normed, pick, router)


def collect(y, mix, stream, depth, size):
    rows, width = stream.shape
    cap = y.shape[2]
    dma = pltpu.SemaphoreType.DMA
    vmem = pl.BlockSpec(memory_space=pltpu.VMEM)
    return pl.pallas_call(
        functools.partial(collect_kernel, depth, size),
        out_shape=jax.ShapeDtypeStruct((rows, width), jnp.bfloat16),
        in_specs=[pl.BlockSpec(memory_space=pl.ANY), vmem, vmem],
        out_specs=vmem,
        scratch_shapes=[
            pltpu.VMEM((depth, size, cap, width), jnp.bfloat16),
            pltpu.VMEM((depth - 1, rows, width), jnp.bfloat16),
            pltpu.VMEM((depth - 1, rows, width), jnp.bfloat16),
            dma((depth - 1,)), dma((depth - 1,)),
            dma((depth, size - 1)), dma((depth, size - 1)), dma((depth,)),
        ],
        compiler_params=pltpu.CompilerParams(
            collective_id=1, has_side_effects=True, vmem_limit_bytes=48 * 1024 * 1024
        ),
        name="collect",
    )(y, mix, stream)


def on_device(
    queries,
    draft_keys,
    draft_values,
    tree_parents,
    cache_keys,
    cache_values,
    cache_lengths,
    prompt_keys,
    prompt_values,
    group_ids,
    residual,
    norm_gain,
    router,
    w_gate,
    w_up,
    w_down,
    expert_ids,
    accepted_rows,
):
    requests, tree_len, width = queries.shape
    row_count = requests * tree_len
    attended, stream, normed = attention(
        queries, draft_keys, draft_values, tree_parents, cache_keys, cache_values, cache_lengths,
        prompt_keys, prompt_values, group_ids, residual, norm_gain,
    )
    attended = attended.reshape(requests, tree_len, width)
    routed = expert_ids.reshape(row_count, TOPK)
    depth, size = lax.axis_size("req"), lax.axis_size("exp")
    all_routed = lax.all_gather(routed, "req", axis=0, tiled=False)
    target = all_routed * CAP + jax.vmap(slot_numbers)(all_routed)
    slots = jnp.arange(EXPERTS * CAP, dtype=jnp.int32).reshape(EXPERTS, CAP)
    pick = (target[:, None, None, :, 0] == slots[None, :, :, None]) | (
        target[:, None, None, :, 1] == slots[None, :, :, None]
    )
    pick = pick.astype(jnp.bfloat16)
    arrived, logits = dispatch(
        normed, pick, jnp.pad(router, ((0, 0), (0, STAT - EXPERTS))), depth, size
    )
    named = all_routed[..., None] == jnp.arange(EXPERTS, dtype=jnp.int32)
    chosen = jnp.sum(jnp.where(named, logits[:, :, None, :EXPERTS], 0.0), axis=-1)
    gate_first = 1.0 / (1.0 + jnp.exp(chosen[..., 1] - chosen[..., 0]))
    all_gates = jnp.stack([gate_first, 1.0 - gate_first], axis=-1)
    hit = target[:, None, :, None, :] == slots[None, :, None, :, None]
    mix = jnp.sum(jnp.where(hit, all_gates[:, None, :, None, :], 0.0), axis=-1)
    mix_high = mix.astype(jnp.bfloat16)
    mix_low = (mix - lax.reduce_precision(mix, 8, 7)).astype(jnp.bfloat16)
    mix = jnp.concatenate([mix_high, mix_low], axis=2)
    row_piece = arrived.reshape(-1, width)
    gate_proj = jnp.dot(row_piece, w_gate[0], preferred_element_type=jnp.float32)
    up_proj = jnp.dot(row_piece, w_up[0], preferred_element_type=jnp.float32)
    hidden = (jax.nn.silu(gate_proj) * up_proj).astype(jnp.bfloat16)
    pieces = jnp.dot(hidden, w_down[0], preferred_element_type=jnp.float32).astype(jnp.bfloat16)
    layer_out = collect(
        pieces.reshape(depth, size, CAP, width), mix, stream, depth, size
    ).reshape(requests, tree_len, width)
    kept_keys = jnp.take_along_axis(draft_keys, accepted_rows[:, :, None], axis=1)
    kept_values = jnp.take_along_axis(draft_values, accepted_rows[:, :, None], axis=1)
    accepted_cache = jnp.stack([kept_keys, kept_values], axis=1)
    return (attended, layer_out, accepted_cache)


def solution(mesh):
    return jax.shard_map(
        on_device,
        mesh=mesh,
        in_specs=(
            P(("req", "exp"), None, None),
            P(("req", "exp"), None, None),
            P(("req", "exp"), None, None),
            P(("req", "exp"), None),
            P(("req", "exp"), None, None),
            P(("req", "exp"), None, None),
            P(("req", "exp")),
            P("req", "exp", None),
            P("req", "exp", None),
            P(("req", "exp")),
            P(("req", "exp"), None, None),
            P(),
            P(),
            P("exp", None, "req"),
            P("exp", None, "req"),
            P("exp", "req", None),
            P(("req", "exp"), None, None),
            P(("req", "exp"), None),
        ),
        out_specs=(
            P(("req", "exp"), None, None),
            P(("req", "exp"), None, None),
            P(("req", "exp"), None, None, None),
        ),
        check_vma=False,
    )
```
